512 devices in a mesh: dp: 64 (over z, y_hi, core), blk: 8 (over y_lo, x).
Axes of the slice: x: 4, y: 4 (y_hi: 2, y_lo: 2; y = y_hi * 2 + y_lo), z: 16, core: 2. Of those that a mesh axis runs over, the one named last changes fastest.
Arguments:
- inputs: bfloat16 [20480, 16384], P('dp', 'blk'), may hold values from -6 to 6
- left_factor: bfloat16 [128, 128, 128], P('blk'), may hold values from -0.5 to 0.5
- right_factor: bfloat16 [128, 128, 128], P('blk'), may hold values from -0.5 to 0.5
- grad_output: bfloat16 [20480, 16384], P('dp', 'blk'), may hold values from -6 to 6
Outputs:
- grad_in: bfloat16 [20480, 16384], P('dp', 'blk')
- grad_left: float32 [128, 128, 128], P('blk', 'dp')
- grad_right: float32 [128, 128, 128], P('blk', 'dp')
The draws below stay inside these ranges and needn't reach their ends.
All inputs are finite; a program needn't handle non-finite values.
Results may differ from the reference program's by a relative error of at most 0.0049.
Values may be sent and summed in bfloat16 or wider, within the bound.
A program may use at most 64 MiB of HBM per device.

```python
import jax
import jax.numpy as jnp
from jax import lax

BLOCK = 128
TOK_DEV = 320
TOKENS = 20480
WIDTH = 16384
N_DP = 64


def level_of(own_key, extent, cuts, low, high):
    loudness = 1.0
    for dim, parts in cuts:
        draws = jax.random.uniform(jax.random.fold_in(jax.random.fold_in(own_key, 6), dim), (parts,), jnp.float32, low / len(cuts), high / len(cuts))
        loudness = loudness * jnp.repeat(jnp.exp(draws), extent[dim] // parts).reshape((-1,) + (1,) * (len(extent) - 1 - dim))
    return loudness


def centred(own_key, shape, spread, most, pieces=(), held_as=jnp.bfloat16):
    values = spread * jax.random.normal(own_key, shape, jnp.float32)
    if pieces:
        values = values * level_of(own_key, shape, pieces, -0.22, 0.18)
    return jnp.clip(values, -most, most).astype(held_as)


def setup_inputs(seed: int = 0) -> dict:
    keys = jax.random.split(jax.random.key(seed), 5)
    inputs = centred(keys[0], (TOKENS, WIDTH), 1.0, 6.0, ((0, 64), (1, 8)))
    left_factor = centred(keys[1], (BLOCK, BLOCK, BLOCK), BLOCK ** -0.5, 0.5, ((0, 8),))
    right_factor = centred(keys[2], (BLOCK, BLOCK, BLOCK), BLOCK ** -0.5, 0.5, ((0, 8),))
    grad_output = centred(keys[3], (TOKENS, WIDTH), 1.0, 6.0, ((0, 64), (1, 8)))
    return dict(inputs=inputs, left_factor=left_factor, right_factor=right_factor, grad_output=grad_output)


def reference(inputs, left_factor, right_factor, grad_output):
    loss_scale = float(TOKENS) ** -0.5
    left_wide = left_factor.astype(jnp.float32)
    right_wide = right_factor.astype(jnp.float32)
    feature_blocks = inputs.reshape(N_DP, TOK_DEV, BLOCK, BLOCK)
    upstream_blocks = grad_output.reshape(N_DP, TOK_DEV, BLOCK, BLOCK)

    def advance(totals, batch_pair):
        feature_rows, upstream_rows = batch_pair
        feature_wide = feature_rows.astype(jnp.float32)
        upstream_wide = upstream_rows.astype(jnp.float32)
        hidden = jnp.einsum("tki,kij->tkj", feature_wide, left_wide).astype(jnp.bfloat16)
        back = jnp.einsum("tjm,jkm->tkj", upstream_wide, right_wide).astype(jnp.bfloat16)
        hidden = lax.optimization_barrier(hidden)
        back = lax.optimization_barrier(back)
        hidden_wide = hidden.astype(jnp.float32)
        back_wide = back.astype(jnp.float32)
        input_grad = jnp.einsum("tkj,kij->tki", back_wide, left_wide).astype(jnp.bfloat16)
        left_total = totals[0] + jnp.einsum("tki,tkj->kij", feature_wide, back_wide)
        right_total = totals[1] + jnp.einsum("tkj,tjm->jkm", hidden_wide, upstream_wide)
        return (left_total, right_total), input_grad.reshape(TOK_DEV, BLOCK * BLOCK)

    empty = jnp.zeros((BLOCK, BLOCK, BLOCK), jnp.float32)
    (left_total, right_total), input_grads = lax.scan(advance, (empty, empty), (feature_blocks, upstream_blocks))
    return input_grads.reshape(TOKENS, WIDTH), left_total * loss_scale, right_total * loss_scale
```

```python
import functools

import jax
import jax.numpy as jnp
from jax import lax
from jax.experimental import pallas as pl
from jax.experimental.pallas import tpu as pltpu
from jax.sharding import PartitionSpec as P

MESH = pl.DeviceIdType.MESH


def reduce_kernel(
    scale, rings, l_ref, r_ref, lo_ref, ro_ref, pair, up, down, fold,
    pair_s, pair_r, up_s, up_r, down_s, down_r, fold_s, fold_r,
):
    me = lax.axis_index("dp")
    core, high, z = lax.rem(me, 2), lax.rem(me // 2, 2), me // 4
    half = rings // 2
    mate = me + 1 - 2 * core
    across = me + 2 - 4 * high
    above = lax.rem(z + 1, rings) * 4 + high * 2 + core
    below = lax.rem(z + rings - 1, rings) * 4 + high * 2 + core
    lanes = (r_ref, l_ref)
    outs = (ro_ref, lo_ref)

    barrier = pltpu.get_barrier_semaphore()
    for peer in (mate, across, above, below):
        pl.semaphore_signal(barrier, inc=1, device_id={"dp": peer}, device_id_type=MESH)
    pl.semaphore_wait(barrier, 4)

    order = []
    for step in range(half):
        order.append(lax.rem(z + half - step, rings))
        if step < half - 1:
            order.append(lax.rem(z + rings - (half - 1 - step), rings))
    order.append(z)

    def send(src, dst, send_sem, recv_sem, peer):
        copy = pltpu.make_async_remote_copy(
            src_ref=src, dst_ref=dst, send_sem=send_sem, recv_sem=recv_sem,
            device_id={"dp": peer}, device_id_type=MESH,
        )
        copy.start()
        return copy

    pairs = [[None] * rings for _ in lanes]
    for k, target in enumerate(order):
        for lane, ref in enumerate(lanes):
            pairs[lane][k] = send(
                ref.at[target, :, 1 - core], pair.at[lane, k],
                pair_s.at[lane, k], pair_r.at[lane, k], mate,
            )

    started = []

    def own(lane, k):
        pairs[lane][k].wait_recv()
        return pair[lane, k] + lanes[lane][order[k], :, core]

    ups, downs = [None, None], [None, None]
    for step in range(half):
        for lane in range(2):
            k = 2 * step
            mine = own(lane, k)
            if step == 0:
                source = pair.at[lane, k]
                source[...] = mine
            else:
                ups[lane].wait_recv()
                source = up.at[lane, step - 1]
                source[...] += mine
            ups[lane] = send(source, up.at[lane, step], up_s.at[lane, step], up_r.at[lane, step], above)
            started.append(ups[lane])
            if step < half - 1:
                k = 2 * step + 1
                mine = own(lane, k)
                if step == 0:
                    source = pair.at[lane, k]
                    source[...] = mine
                else:
                    downs[lane].wait_recv()
                    source = down.at[lane, step - 1]
                    source[...] += mine
                downs[lane] = send(
                    source, down.at[lane, step], down_s.at[lane, step], down_r.at[lane, step], below
                )
                started.append(downs[lane])

    folds = []
    for lane in range(2):
        mine = own(lane, rings - 1)
        ups[lane].wait_recv()
        downs[lane].wait_recv()
        pair[lane, rings - 1] = mine + up[lane, half - 1] + down[lane, half - 2]
        folds.append(
            send(pair.at[lane, rings - 1, 1 - high], fold.at[lane], fold_s.at[lane], fold_r.at[lane], across)
        )
    for lane in range(2):
        folds[lane].wait_recv()
        outs[lane][...] = (pair[lane, rings - 1, high] + fold[lane]) * scale
    for copies in (*pairs, started, folds):
        for copy in copies:
            copy.wait_send()


def reduce_both(left_term, right_term, scale, replicas):
    owned, width, _ = left_term.shape
    rings = replicas // 4
    half = rings // 2
    rows = owned * (width // replicas)

    def arrange(term):
        return jnp.transpose(term, (1, 0, 2)).reshape(rings, 2, 2, rows, width)

    dma = pltpu.SemaphoreType.DMA
    vmem = pl.BlockSpec(memory_space=pltpu.VMEM)
    piece = (2, rows, width)
    left, right = pl.pallas_call(
        functools.partial(reduce_kernel, scale, rings),
        out_shape=[jax.ShapeDtypeStruct((rows, width), jnp.float32)] * 2,
        in_specs=[vmem, vmem],
        out_specs=[vmem, vmem],
        scratch_shapes=[
            pltpu.VMEM((2, rings) + piece, jnp.float32),
            pltpu.VMEM((2, half) + piece, jnp.float32),
            pltpu.VMEM((2, half - 1) + piece, jnp.float32),
            pltpu.VMEM((2, rows, width), jnp.float32),
            dma((2, rings)), dma((2, rings)),
            dma((2, half)), dma((2, half)),
            dma((2, half - 1)), dma((2, half - 1)),
            dma((2,)), dma((2,)),
        ],
        compiler_params=pltpu.CompilerParams(collective_id=0, has_side_effects=True),
        name="reduce_over_dp",
    )(arrange(left_term), arrange(right_term))

    def restore(out):
        return jnp.transpose(out.reshape(width // replicas, owned, width), (1, 0, 2))

    return restore(left), restore(right)


def local(inputs, left_factor, right_factor, grad_output):
    groups = lax.axis_size("blk")
    replicas = lax.axis_size("dp")
    tokens_here = inputs.shape[0]
    owned = left_factor.shape[0]
    width_block = left_factor.shape[1]
    loss_scale = float(tokens_here * replicas) ** (-0.5)
    features = inputs.reshape(tokens_here, owned, width_block)
    upstream = grad_output.reshape(tokens_here, owned, width_block)
    left_view = left_factor.reshape(owned, width_block, groups, owned)
    right_view = right_factor.reshape(owned, groups, owned, width_block)
    hidden = jnp.einsum("tci,cibj->btcj", features, left_view, preferred_element_type=jnp.float32)
    hidden_send = hidden.astype(jnp.bfloat16).reshape(groups, tokens_here, owned * owned)
    back = jnp.einsum("tjm,jbcm->btcj", upstream, right_view, preferred_element_type=jnp.float32)
    back_send = back.astype(jnp.bfloat16).reshape(groups, tokens_here, owned * owned)
    hidden_recv = lax.all_to_all(hidden_send, "blk", split_axis=0, concat_axis=0, tiled=True)
    hidden_four = hidden_recv.reshape(groups, tokens_here, owned, owned)
    right_term = jnp.einsum(
        "btcj,tjm->jbcm", hidden_four, upstream, preferred_element_type=jnp.float32
    )
    right_term = right_term.reshape(owned, groups * owned, width_block)
    piece = lax.all_to_all(back_send, "blk", split_axis=0, concat_axis=0, tiled=True)
    count = piece.shape[1]
    piece_four = piece.reshape(groups, count, owned, owned)
    grad_piece = jnp.einsum(
        "btcj,cibj->tci", piece_four, left_view, preferred_element_type=jnp.float32
    )
    grad_piece = grad_piece.astype(jnp.bfloat16).reshape(count, owned * width_block)
    token_major = jnp.transpose(piece_four, (1, 0, 2, 3))
    left_term = jnp.einsum(
        "tci,tbcj->cibj", features, token_major, preferred_element_type=jnp.float32
    )
    left_term = left_term.reshape(owned, width_block, groups * owned)
    left_summed, right_summed = reduce_both(left_term, right_term, loss_scale, replicas)
    return (grad_piece, left_summed, right_summed)


def solution(mesh):
    return jax.shard_map(
        local,
        mesh=mesh,
        in_specs=(P("dp", "blk"), P("blk", None, None), P("blk", None, None), P("dp", "blk")),
        out_specs=(P("dp", "blk"), P("blk", "dp", None), P("blk", "dp", None)),
        check_vma=False,
    )
```

```python
import functools

import jax
import jax.numpy as jnp
from jax import lax
from jax.experimental import pallas as pl
from jax.experimental.pallas import tpu as pltpu
from jax.sharding import PartitionSpec as P

MESH = pl.DeviceIdType.MESH
OFFSETS = ((2, 1), (2, 0), (1, 1), (3, 1), (1, 0), (3, 0), (0, 1))
NN = (((1,), (0,)), ((), ()))
NT = (((1,), (1,)), ((), ()))
TN = (((0,), (0,)), ((), ()))


def dot(a, b, dims):
    return lax.dot_general(a, b, dims, preferred_element_type=jnp.float32)


def swapped(index):
    return (index & ~6) | ((index & 4) >> 1) | ((index & 2) << 1)


def one_hot(rows, pick):
    row = lax.broadcasted_iota(jnp.int32, (rows, rows), 0)
    col = lax.broadcasted_iota(jnp.int32, (rows, rows), 1)
    return jnp.where(col == pick(row), 1.0, 0.0).astype(jnp.bfloat16)


def monarch_kernel(
    scale, rings, x_ref, l_ref, r_ref, g_ref, gin_ref, lo_ref, ro_ref,
    hc, hs, hr, bc, bs, br, xt, lt, sr, sl, pair, up, down, fold,
    hid_s, hid_r, back_s, back_r,
    pair_s, pair_r, up_s, up_r, down_s, down_r, fold_s, fold_r,
):
    owned, width = l_ref.shape[0], l_ref.shape[1]
    tokens = x_ref.shape[0]
    me = lax.axis_index("dp")
    core, high, z = lax.rem(me, 2), lax.rem(me // 2, 2), me // 4
    half = rings // 2
    mate = me + 1 - 2 * core
    across = me + 2 - 4 * high
    above = lax.rem(z + 1, rings) * 4 + high * 2 + core
    below = lax.rem(z + rings - 1, rings) * 4 + high * 2 + core
    blk = lax.axis_index("blk")
    blk_y, blk_x = blk // 4, lax.rem(blk, 4)
    partners = [
        lax.rem(blk_y + dy, 2) * 4 + lax.rem(blk_x + dx, 4) for dx, dy in OFFSETS
    ]

    barrier = pltpu.get_barrier_semaphore()
    for peer in (mate, across, above, below):
        pl.semaphore_signal(barrier, inc=1, device_id={"dp": peer}, device_id_type=MESH)
    for peer in partners:
        pl.semaphore_signal(barrier, inc=1, device_id={"blk": peer}, device_id_type=MESH)

    def send(src, dst, send_sem, recv_sem, axis, peer):
        copy = pltpu.make_async_remote_copy(
            src_ref=src, dst_ref=dst, send_sem=send_sem, recv_sem=recv_sem,
            device_id={axis: peer}, device_id_type=MESH,
        )
        copy.start()
        return copy

    def columns(c):
        return pl.ds(pl.multiple_of(c * width, width), width)

    def split(value):
        return value.astype(jnp.bfloat16).reshape(width // owned, owned, tokens)

    def hidden_block(c, carry):
        lt[c] = l_ref[c].T
        hc[:, c] = split(dot(lt[c], x_ref[:, columns(c)], NT))
        return carry

    def back_block(j, carry):
        bc[:, j] = split(dot(r_ref[j], g_ref[:, columns(j)], NT))
        return carry

    def exchange(blocks, staged, landed, order, send_sem, recv_sem):
        copies = []
        for n, peer in enumerate((*partners, blk)):
            rows = blocks[peer].reshape(owned * owned, tokens)
            moved = dot(order, rows, NN).astype(jnp.bfloat16).reshape(owned, owned, tokens)
            if n < len(partners):
                staged[n] = moved
                copies.append(
                    send(staged.at[n], landed.at[:, blk], send_sem.at[n], recv_sem.at[n], "blk", peer)
                )
            else:
                landed[:, blk] = moved
        return copies

    lax.fori_loop(0, owned, hidden_block, 0, unroll=2)
    to_right = one_hot(owned * owned, lambda r: (swapped(r & 15) << 4) | (r >> 4))
    pl.semaphore_wait(barrier, 4 + len(partners))
    hidden_copies = exchange(hc, hs, hr, to_right, hid_s, hid_r)
    lax.fori_loop(0, owned, back_block, 0, unroll=2)
    to_left = one_hot(owned * owned, lambda r: ((r & 15) << 4) | (r >> 4))
    back_copies = exchange(bc, bs, br, to_left, back_s, back_r)

    turn = one_hot(width, swapped)

    def turn_block(c, carry):
        xt[c] = dot(turn, x_ref[:, columns(c)], NT).astype(jnp.bfloat16)
        return carry

    lax.fori_loop(0, owned, turn_block, 0, unroll=2)

    order = []
    for step in range(half):
        order.append(lax.rem(z + half - step, rings))
        if step < half - 1:
            order.append(lax.rem(z + rings - (half - 1 - step), rings))
    order.append(z)
    piece = owned * 4

    def reduce_lane(lane, ref, out, between):
        def part(target, which):
            return pl.ds(pl.multiple_of(target * (2 * piece) + which * piece, piece), piece)

        pairs = [
            send(
                ref.at[part(target, 1 - core)], pair.at[lane, k],
                pair_s.at[lane, k], pair_r.at[lane, k], "dp", mate,
            )
            for k, target in enumerate(order)
        ]
        started = list(pairs)

        def own(k):
            pairs[k].wait_recv()
            return pair[lane, k] + ref[part(order[k], core)]

        def advance(step, k, before, held, send_sem, recv_sem, peer):
            mine = own(k)
            if step == 0:
                source = pair.at[lane, k]
                source[...] = mine
            else:
                before.wait_recv()
                source = held.at[lane, step - 1]
                source[...] += mine
            copy = send(
                source, held.at[lane, step], send_sem.at[lane, step], recv_sem.at[lane, step], "dp", peer
            )
            started.append(copy)
            return copy

        rise = sink = None
        for step in range(half):
            rise = advance(step, 2 * step, rise, up, up_s, up_r, above)
            if step < half - 1:
                sink = advance(step, 2 * step + 1, sink, down, down_s, down_r, below)
            between(step)
        mine = own(rings - 1)
        rise.wait_recv()
        sink.wait_recv()
        last = pair.at[lane, rings - 1]
        last[...] = mine + up[lane, half - 1] + down[lane, half - 2]

        def part_of(which):
            return pl.ds(pl.multiple_of(which * (piece // 2), piece // 2), piece // 2)

        folded = send(
            last.at[part_of(1 - high)], fold.at[lane], fold_s.at[lane], fold_r.at[lane], "dp", across
        )
        started.append(folded)

        def finish():
            folded.wait_recv()
            out[...] = (last[part_of(high)] + fold[lane]) * scale
            for copy in started:
                copy.wait_send()

        return finish

    for copy in hidden_copies:
        copy.wait_recv()
    for j in range(owned):
        sr[pl.ds(j, width, stride=owned), :] = dot(
            hr[j].reshape(width, tokens), g_ref[:, j * width:(j + 1) * width], NN
        )
    finish_right = reduce_lane(0, sr, ro_ref, lambda step: None)

    for copy in back_copies:
        copy.wait_recv()
    for c in range(owned):
        sl[pl.ds(c, width, stride=owned), :] = dot(xt[c], br[c].reshape(width, tokens), NT)

    def grad_in(step):
        for c in range(2 * step, 2 * step + 2):
            gin_ref[:, c * width:(c + 1) * width] = dot(
                br[c].reshape(width, tokens), lt[c], TN
            ).astype(jnp.bfloat16)

    finish_left = reduce_lane(1, sl, lo_ref, grad_in)
    finish_right()
    finish_left()
    for copy in (*hidden_copies, *back_copies):
        copy.wait_send()


def local(inputs, left_factor, right_factor, grad_output):
    replicas = lax.axis_size("dp")
    groups = lax.axis_size("blk")
    tokens = inputs.shape[0]
    owned, width = left_factor.shape[0], left_factor.shape[1]
    scale = float(tokens * replicas) ** (-0.5)
    rings = replicas // 4
    half = rings // 2
    rows = owned * (width // replicas)
    dma = pltpu.SemaphoreType.DMA
    vmem = pl.BlockSpec(memory_space=pltpu.VMEM)
    bf16, f32 = jnp.bfloat16, jnp.float32
    grad, left, right = pl.pallas_call(
        functools.partial(monarch_kernel, scale, rings),
        out_shape=[
            jax.ShapeDtypeStruct(inputs.shape, bf16),
            jax.ShapeDtypeStruct((rows, width), f32),
            jax.ShapeDtypeStruct((rows, width), f32),
        ],
        in_specs=[vmem] * 4,
        out_specs=[vmem] * 3,
        scratch_shapes=[
            pltpu.VMEM((groups, owned, owned, tokens), bf16),
            pltpu.VMEM((groups - 1, owned, owned, tokens), bf16),
            pltpu.VMEM((owned, groups, owned, tokens), bf16),
            pltpu.VMEM((groups, owned, owned, tokens), bf16),
            pltpu.VMEM((groups - 1, owned, owned, tokens), bf16),
            pltpu.VMEM((owned, groups, owned, tokens), bf16),
            pltpu.VMEM((owned, width, tokens), bf16),
            pltpu.VMEM((owned, width, width), bf16),
            pltpu.VMEM((owned * width, width), f32),
            pltpu.VMEM((owned * width, width), f32),
            pltpu.VMEM((2, rings, 2 * rows, width), f32),
            pltpu.VMEM((2, half, 2 * rows, width), f32),
            pltpu.VMEM((2, half - 1, 2 * rows, width), f32),
            pltpu.VMEM((2, rows, width), f32),
            dma((groups - 1,)), dma((groups - 1,)), dma((groups - 1,)), dma((groups - 1,)),
            dma((2, rings)), dma((2, rings)),
            dma((2, half)), dma((2, half)),
            dma((2, half - 1)), dma((2, half - 1)),
            dma((2,)), dma((2,)),
        ],
        compiler_params=pltpu.CompilerParams(
            collective_id=0, has_side_effects=True, vmem_limit_bytes=58 * 1024 * 1024
        ),
        name="monarch_backward",
    )(inputs, left_factor, right_factor, grad_output)

    def restore(out):
        return jnp.transpose(out.reshape(width // replicas, owned, width), (1, 0, 2))

    return grad, restore(left), restore(right)


def solution(mesh):
    return jax.shard_map(
        local,
        mesh=mesh,
        in_specs=(P("dp", "blk"), P("blk", None, None), P("blk", None, None), P("dp", "blk")),
        out_specs=(P("dp", "blk"), P("blk", "dp", None), P("blk", "dp", None)),
        check_vma=False,
    )
```

```python
import functools

import jax
import jax.numpy as jnp
from jax import lax
from jax.experimental import pallas as pl
from jax.experimental.pallas import tpu as pltpu
from jax.sharding import PartitionSpec as P

MESH = pl.DeviceIdType.MESH
OFFSETS = ((2, 1), (2, 0), (1, 1), (3, 1), (1, 0), (3, 0), (0, 1))
LEAD = 5
NN = (((1,), (0,)), ((), ()))
NT = (((1,), (1,)), ((), ()))
TN = (((0,), (0,)), ((), ()))


def dot(a, b, dims):
    return lax.dot_general(a, b, dims, preferred_element_type=jnp.float32)


def swapped(index):
    return (index & ~6) | ((index & 4) >> 1) | ((index & 2) << 1)


def one_hot(rows, pick):
    row = lax.broadcasted_iota(jnp.int32, (rows, rows), 0)
    col = lax.broadcasted_iota(jnp.int32, (rows, rows), 1)
    return jnp.where(col == pick(row), 1.0, 0.0).astype(jnp.bfloat16)


def monarch_kernel(
    scale, rings, x_ref, l_ref, r_ref, g_ref, gin_ref, lo_ref, ro_ref,
    hc, hs, hr, bc, bs, br, xt, lt, sr, sl, pair, up, down, fold,
    hid_s, hid_r, back_s, back_r,
    pair_s, pair_r, up_s, up_r, down_s, down_r, fold_s, fold_r,
):
    owned, width = l_ref.shape[0], l_ref.shape[1]
    tokens = x_ref.shape[0]
    me = lax.axis_index("dp")
    core, high, z = lax.rem(me, 2), lax.rem(me // 2, 2), me // 4
    half = rings // 2
    mate = me + 1 - 2 * core
    across = me + 2 - 4 * high
    above = lax.rem(z + 1, rings) * 4 + high * 2 + core
    below = lax.rem(z + rings - 1, rings) * 4 + high * 2 + core
    blk = lax.axis_index("blk")
    blk_y, blk_x = blk // 4, lax.rem(blk, 4)
    partners = [
        lax.rem(blk_y + dy, 2) * 4 + lax.rem(blk_x + dx, 4) for dx, dy in OFFSETS
    ]

    barrier = pltpu.get_barrier_semaphore()
    for peer in (mate, across, above, below):
        pl.semaphore_signal(barrier, inc=1, device_id={"dp": peer}, device_id_type=MESH)
    for peer in partners:
        pl.semaphore_signal(barrier, inc=1, device_id={"blk": peer}, device_id_type=MESH)

    def send(src, dst, send_sem, recv_sem, axis, peer):
        copy = pltpu.make_async_remote_copy(
            src_ref=src, dst_ref=dst, send_sem=send_sem, recv_sem=recv_sem,
            device_id={axis: peer}, device_id_type=MESH,
        )
        copy.start()
        return copy

    def columns(c):
        return pl.ds(pl.multiple_of(c * width, width), width)

    def split(value):
        return value.astype(jnp.bfloat16).reshape(width // owned, owned, tokens)

    def hidden_block(c, carry):
        lt[c] = l_ref[c].T
        hc[:, c] = split(dot(lt[c], x_ref[:, columns(c)], NT))
        return carry

    def back_block(j, carry):
        bc[:, j] = split(dot(r_ref[j], g_ref[:, columns(j)], NT))
        return carry

    def exchange(blocks, staged, landed, order, send_sem, recv_sem):
        copies = []
        for n, peer in enumerate((*partners, blk)):
            rows = blocks[peer].reshape(owned * owned, tokens)
            moved = dot(order, rows, NN).astype(jnp.bfloat16).reshape(owned, owned, tokens)
            if n < len(partners):
                staged[n] = moved
                copies.append(
                    send(staged.at[n], landed.at[:, blk], send_sem.at[n], recv_sem.at[n], "blk", peer)
                )
            else:
                landed[:, blk] = moved
        return copies

    lax.fori_loop(0, owned, hidden_block, 0, unroll=2)
    to_right = one_hot(owned * owned, lambda r: (swapped(r & 15) << 4) | (r >> 4))
    pl.semaphore_wait(barrier, 4 + len(partners))
    hidden_copies = exchange(hc, hs, hr, to_right, hid_s, hid_r)
    lax.fori_loop(0, owned, back_block, 0, unroll=2)
    to_left = one_hot(owned * owned, lambda r: ((r & 15) << 4) | (r >> 4))
    back_copies = exchange(bc, bs, br, to_left, back_s, back_r)

    turn = one_hot(width, swapped)

    def turn_block(c, carry):
        xt[c] = dot(turn, x_ref[:, columns(c)], NT).astype(jnp.bfloat16)
        return carry

    lax.fori_loop(0, owned, turn_block, 0, unroll=2)

    order = []
    for step in range(half):
        order.append(lax.rem(z + half - step, rings))
        if step < half - 1:
            order.append(lax.rem(z + rings - (half - 1 - step), rings))
    order.append(z)
    piece = owned * 4

    halves = (1 - high, high)
    slab = piece // 2

    def rows_at(start, count):
        return pl.ds(pl.multiple_of(start, count), count)

    def reduce_lane(lane, ref, out):
        pairs = [
            send(
                ref.at[rows_at(target * (2 * piece) + (1 - core) * piece, piece)], pair.at[lane, k],
                pair_s.at[lane, k], pair_r.at[lane, k], "dp", mate,
            )
            for k, target in enumerate(order)
        ]
        started = list(pairs)

        def own(k, e):
            if e == 0:
                pairs[k].wait_recv()
            start = order[k] * (2 * piece) + core * piece + halves[e] * slab
            return pair[lane, k, rows_at(halves[e] * slab, slab)] + ref[rows_at(start, slab)]

        def advance(step, k, e, before, held, send_sem, recv_sem, peer):
            mine = own(k, e)
            if step == 0:
                source = pair.at[lane, k, rows_at(halves[e] * slab, slab)]
                source[...] = mine
            else:
                before.wait_recv()
                source = held.at[lane, e, step - 1]
                source[...] += mine
            copy = send(
                source, held.at[lane, e, step],
                send_sem.at[lane, e, step], recv_sem.at[lane, e, step], "dp", peer,
            )
            started.append(copy)
            return copy

        rise, sink = [None, None], [None, None]
        for step in range(half):
            for e in range(2):
                rise[e] = advance(step, 2 * step, e, rise[e], up, up_s, up_r, above)
                if step < half - 1:
                    sink[e] = advance(step, 2 * step + 1, e, sink[e], down, down_s, down_r, below)
            yield
        last = pair.at[lane, rings - 1]
        for e in range(2):
            mine = own(rings - 1, e)
            rise[e].wait_recv()
            sink[e].wait_recv()
            total = last.at[rows_at(halves[e] * slab, slab)]
            total[...] = mine + up[lane, e, half - 1] + down[lane, e, half - 2]
            if e == 0:
                folded = send(total, fold.at[lane], fold_s.at[lane], fold_r.at[lane], "dp", across)
                started.append(folded)
        yield
        folded.wait_recv()
        out[...] = (last[rows_at(high * slab, slab)] + fold[lane]) * scale
        for copy in started:
            copy.wait_send()
        yield

    for copy in hidden_copies:
        copy.wait_recv()
    for j in range(owned):
        sr[pl.ds(j, width, stride=owned), :] = dot(
            hr[j].reshape(width, tokens), g_ref[:, j * width:(j + 1) * width], NN
        )
    right_lane = reduce_lane(0, sr, ro_ref)
    for _ in range(LEAD):
        next(right_lane)

    for copy in back_copies:
        copy.wait_recv()
    for c in range(owned):
        sl[pl.ds(c, width, stride=owned), :] = dot(xt[c], br[c].reshape(width, tokens), NT)

    def grad_in(step):
        for c in range(2 * step, 2 * step + 2):
            gin_ref[:, c * width:(c + 1) * width] = dot(
                br[c].reshape(width, tokens), lt[c], TN
            ).astype(jnp.bfloat16)

    left_lane = reduce_lane(1, sl, lo_ref)
    for step in range(half + 2):
        if step + LEAD < half + 2:
            next(right_lane)
        next(left_lane)
        if step < half:
            grad_in(step)
    for copy in (*hidden_copies, *back_copies):
        copy.wait_send()


def local(inputs, left_factor, right_factor, grad_output):
    replicas = lax.axis_size("dp")
    groups = lax.axis_size("blk")
    tokens = inputs.shape[0]
    owned, width = left_factor.shape[0], left_factor.shape[1]
    scale = float(tokens * replicas) ** (-0.5)
    rings = replicas // 4
    half = rings // 2
    rows = owned * (width // replicas)
    dma = pltpu.SemaphoreType.DMA
    vmem = pl.BlockSpec(memory_space=pltpu.VMEM)
    bf16, f32 = jnp.bfloat16, jnp.float32
    grad, left, right = pl.pallas_call(
        functools.partial(monarch_kernel, scale, rings),
        out_shape=[
            jax.ShapeDtypeStruct(inputs.shape, bf16),
            jax.ShapeDtypeStruct((rows, width), f32),
            jax.ShapeDtypeStruct((rows, width), f32),
        ],
        in_specs=[vmem] * 4,
        out_specs=[vmem] * 3,
        scratch_shapes=[
            pltpu.VMEM((groups, owned, owned, tokens), bf16),
            pltpu.VMEM((groups - 1, owned, owned, tokens), bf16),
            pltpu.VMEM((owned, groups, owned, tokens), bf16),
            pltpu.VMEM((groups, owned, owned, tokens), bf16),
            pltpu.VMEM((groups - 1, owned, owned, tokens), bf16),
            pltpu.VMEM((owned, groups, owned, tokens), bf16),
            pltpu.VMEM((owned, width, tokens), bf16),
            pltpu.VMEM((owned, width, width), bf16),
            pltpu.VMEM((owned * width, width), f32),
            pltpu.VMEM((owned * width, width), f32),
            pltpu.VMEM((2, rings, 2 * rows, width), f32),
            pltpu.VMEM((2, 2, half, rows, width), f32),
            pltpu.VMEM((2, 2, half - 1, rows, width), f32),
            pltpu.VMEM((2, rows, width), f32),
            dma((groups - 1,)), dma((groups - 1,)), dma((groups - 1,)), dma((groups - 1,)),
            dma((2, rings)), dma((2, rings)),
            dma((2, 2, half)), dma((2, 2, half)),
            dma((2, 2, half - 1)), dma((2, 2, half - 1)),
            dma((2,)), dma((2,)),
        ],
        compiler_params=pltpu.CompilerParams(
            collective_id=0, has_side_effects=True, vmem_limit_bytes=58 * 1024 * 1024
        ),
        name="monarch_backward",
    )(inputs, left_factor, right_factor, grad_output)

    def restore(out):
        return jnp.transpose(out.reshape(width // replicas, owned, width), (1, 0, 2))

    return grad, restore(left), restore(right)


def solution(mesh):
    return jax.shard_map(
        local,
        mesh=mesh,
        in_specs=(P("dp", "blk"), P("blk", None, None), P("blk", None, None), P("dp", "blk")),
        out_specs=(P("dp", "blk"), P("blk", "dp", None), P("blk", "dp", None)),
        check_vma=False,
    )
```

```python
import functools

import jax
import jax.numpy as jnp
from jax import lax
from jax.experimental import pallas as pl
from jax.experimental.pallas import tpu as pltpu
from jax.sharding import PartitionSpec as P

MESH = pl.DeviceIdType.MESH
OFFSETS = ((2, 1), (2, 0), (1, 1), (3, 1), (1, 0), (3, 0), (0, 1))
LEAD = 5
NN = (((1,), (0,)), ((), ()))
NT = (((1,), (1,)), ((), ()))
TN = (((0,), (0,)), ((), ()))


def dot(a, b, dims):
    return lax.dot_general(a, b, dims, preferred_element_type=jnp.float32)


def swapped(index):
    return (index & ~6) | ((index & 4) >> 1) | ((index & 2) << 1)


def one_hot(rows, pick):
    row = lax.broadcasted_iota(jnp.int32, (rows, rows), 0)
    col = lax.broadcasted_iota(jnp.int32, (rows, rows), 1)
    return jnp.where(col == pick(row), 1.0, 0.0).astype(jnp.bfloat16)


def monarch_kernel(
    scale, rings, x_ref, l_ref, r_ref, g_ref, gin_ref, lo_ref, ro_ref,
    hc, hs, hs_end, hr, hr_end, bc, bs, bs_end, br, br_end, xt, lt, sr, sl, pair, up, down, fold,
    hid_s, hid_r, back_s, back_r,
    pair_s, pair_r, up_s, up_r, down_s, down_r, fold_s, fold_r,
):
    owned, width = l_ref.shape[0], l_ref.shape[1]
    tokens = x_ref.shape[0]
    body = hr.shape[-1]
    rest = tokens - body
    me = lax.axis_index("dp")
    core, high, z = lax.rem(me, 2), lax.rem(me // 2, 2), me // 4
    half = rings // 2
    mate = me + 1 - 2 * core
    across = me + 2 - 4 * high
    above = lax.rem(z + 1, rings) * 4 + high * 2 + core
    below = lax.rem(z + rings - 1, rings) * 4 + high * 2 + core
    blk = lax.axis_index("blk")
    blk_y, blk_x = blk // 4, lax.rem(blk, 4)
    partners = [
        lax.rem(blk_y + dy, 2) * 4 + lax.rem(blk_x + dx, 4) for dx, dy in OFFSETS
    ]

    barrier = pltpu.get_barrier_semaphore()
    for peer in (mate, across, above, below):
        pl.semaphore_signal(barrier, inc=1, device_id={"dp": peer}, device_id_type=MESH)
    for peer in partners:
        pl.semaphore_signal(barrier, inc=1, device_id={"blk": peer}, device_id_type=MESH)

    def send(src, dst, send_sem, recv_sem, axis, peer):
        copy = pltpu.make_async_remote_copy(
            src_ref=src, dst_ref=dst, send_sem=send_sem, recv_sem=recv_sem,
            device_id={axis: peer}, device_id_type=MESH,
        )
        copy.start()
        return copy

    def columns(c):
        return pl.ds(pl.multiple_of(c * width, width), width)

    def split(value):
        return value.astype(jnp.bfloat16).reshape(width // owned, owned, tokens)

    def hidden_block(c, carry):
        lt[c] = l_ref[c].T
        hc[:, c] = split(dot(lt[c], x_ref[:, columns(c)], NT))
        return carry

    def back_block(j, carry):
        bc[:, j] = split(dot(r_ref[j], g_ref[:, columns(j)], NT))
        return carry

    def exchange(blocks, staged, landed, order, send_sem, recv_sem):
        copies = []
        for n, peer in enumerate((*partners, blk)):
            rows = blocks[peer].reshape(owned * owned, tokens)
            moved = dot(order, rows, NN)
            ends = jnp.concatenate([moved[:width, body:], moved[width:, body:]], axis=1)
            pieces = (
                moved[:, :body].astype(jnp.bfloat16).reshape(owned, owned, body),
                ends.astype(jnp.bfloat16).reshape(owned // 2, owned, 2 * rest),
            )
            for part, value in enumerate(pieces):
                if n < len(partners):
                    staged[part][n] = value
                    copies.append(
                        send(
                            staged[part].at[n], landed[part].at[:, blk],
                            send_sem.at[part, n], recv_sem.at[part, n], "blk", peer,
                        )
                    )
                else:
                    landed[part][:, blk] = value
        return copies

    def spread(value, block):
        blank = jnp.zeros_like(value)
        return jnp.concatenate([value, blank] if block < owned // 2 else [blank, value], axis=0)

    lax.fori_loop(0, owned, hidden_block, 0, unroll=2)
    to_right = one_hot(owned * owned, lambda r: (swapped(r & 15) << 4) | (r >> 4))
    pl.semaphore_wait(barrier, 4 + len(partners))
    hidden_copies = exchange(hc, (hs, hs_end), (hr, hr_end), to_right, hid_s, hid_r)
    lax.fori_loop(0, owned, back_block, 0, unroll=2)
    to_left = one_hot(owned * owned, lambda r: ((r & 15) << 4) | (r >> 4))
    back_copies = exchange(bc, (bs, bs_end), (br, br_end), to_left, back_s, back_r)

    turn = one_hot(width, swapped)

    def turn_block(n, carry):
        for first in (0, owned // 2):
            c = n + first
            rows = jnp.concatenate([x_ref[:body, columns(c)], spread(x_ref[body:, columns(c)], first)], axis=0)
            xt[c] = dot(turn, rows, NT).astype(jnp.bfloat16)
        return carry

    lax.fori_loop(0, owned // 2, turn_block, 0)

    order = []
    for step in range(half):
        order.append(lax.rem(z + half - step, rings))
        if step < half - 1:
            order.append(lax.rem(z + rings - (half - 1 - step), rings))
    order.append(z)
    piece = owned * 4

    halves = (1 - high, high)
    slab = piece // 2

    def rows_at(start, count):
        return pl.ds(pl.multiple_of(start, count), count)

    def reduce_lane(lane, ref, out):
        pairs = [
            send(
                ref.at[rows_at(target * (2 * piece) + (1 - core) * piece, piece)], pair.at[lane, k],
                pair_s.at[lane, k], pair_r.at[lane, k], "dp", mate,
            )
            for k, target in enumerate(order)
        ]
        started = list(pairs)

        def own(k, e):
            if e == 0:
                pairs[k].wait_recv()
            start = order[k] * (2 * piece) + core * piece + halves[e] * slab
            return pair[lane, k, rows_at(halves[e] * slab, slab)] + ref[rows_at(start, slab)]

        def advance(step, k, e, before, held, send_sem, recv_sem, peer):
            mine = own(k, e)
            if step == 0:
                source = pair.at[lane, k, rows_at(halves[e] * slab, slab)]
                source[...] = mine
            else:
                before.wait_recv()
                source = held.at[lane, e, step - 1]
                source[...] += mine
            copy = send(
                source, held.at[lane, e, step],
                send_sem.at[lane, e, step], recv_sem.at[lane, e, step], "dp", peer,
            )
            started.append(copy)
            return copy

        rise, sink = [None, None], [None, None]
        for step in range(half):
            for e in range(2):
                rise[e] = advance(step, 2 * step, e, rise[e], up, up_s, up_r, above)
                if step < half - 1:
                    sink[e] = advance(step, 2 * step + 1, e, sink[e], down, down_s, down_r, below)
            yield
        last = pair.at[lane, rings - 1]
        for e in range(2):
            mine = own(rings - 1, e)
            rise[e].wait_recv()
            sink[e].wait_recv()
            total = last.at[rows_at(halves[e] * slab, slab)]
            total[...] = mine + up[lane, e, half - 1] + down[lane, e, half - 2]
            if e == 0:
                folded = send(total, fold.at[lane], fold_s.at[lane], fold_r.at[lane], "dp", across)
                started.append(folded)
        yield
        folded.wait_recv()
        out[...] = (last[rows_at(high * slab, slab)] + fold[lane]) * scale
        for copy in started:
            copy.wait_send()
        yield

    for copy in hidden_copies:
        copy.wait_recv()
    for j in range(owned):
        across_j = slice(j * width, (j + 1) * width)
        ends = hr_end[j % (owned // 2)].reshape(width, 2 * rest)
        sr[pl.ds(j, width, stride=owned), :] = dot(
            hr[j].reshape(width, body), g_ref[:body, across_j], NN
        ) + dot(ends, spread(g_ref[body:, across_j], j), NN)
    right_lane = reduce_lane(0, sr, ro_ref)
    for _ in range(LEAD):
        next(right_lane)

    for copy in back_copies:
        copy.wait_recv()
    for c in range(owned):
        ends = br_end[c % (owned // 2)].reshape(width, 2 * rest)
        sl[pl.ds(c, width, stride=owned), :] = dot(
            xt[c, :, :body], br[c].reshape(width, body), NT
        ) + dot(xt[c, :, body:], ends, NT)

    def grad_in(step):
        for c in range(2 * step, 2 * step + 2):
            across_c = slice(c * width, (c + 1) * width)
            gin_ref[:body, across_c] = dot(br[c].reshape(width, body), lt[c], TN).astype(jnp.bfloat16)
            ends = dot(br_end[c % (owned // 2)].reshape(width, 2 * rest), lt[c], TN)
            first = c // (owned // 2) * rest
            gin_ref[body:, across_c] = ends[first:first + rest].astype(jnp.bfloat16)

    left_lane = reduce_lane(1, sl, lo_ref)
    for step in range(half + 2):
        if step + LEAD < half + 2:
            next(right_lane)
        next(left_lane)
        if step < half:
            grad_in(step)
    for copy in (*hidden_copies, *back_copies):
        copy.wait_send()


def local(inputs, left_factor, right_factor, grad_output):
    replicas = lax.axis_size("dp")
    groups = lax.axis_size("blk")
    tokens = inputs.shape[0]
    owned, width = left_factor.shape[0], left_factor.shape[1]
    scale = float(tokens * replicas) ** (-0.5)
    rings = replicas // 4
    half = rings // 2
    body = tokens - width // 2
    rows = owned * (width // replicas)
    dma = pltpu.SemaphoreType.DMA
    vmem = pl.BlockSpec(memory_space=pltpu.VMEM)
    bf16, f32 = jnp.bfloat16, jnp.float32
    grad, left, right = pl.pallas_call(
        functools.partial(monarch_kernel, scale, rings),
        out_shape=[
            jax.ShapeDtypeStruct(inputs.shape, bf16),
            jax.ShapeDtypeStruct((rows, width), f32),
            jax.ShapeDtypeStruct((rows, width), f32),
        ],
        in_specs=[vmem] * 4,
        out_specs=[vmem] * 3,
        scratch_shapes=[
            pltpu.VMEM((groups, owned, owned, tokens), bf16),
            pltpu.VMEM((groups - 1, owned, owned, body), bf16),
            pltpu.VMEM((groups - 1, owned // 2, owned, width), bf16),
            pltpu.VMEM((owned, groups, owned, body), bf16),
            pltpu.VMEM((owned // 2, groups, owned, width), bf16),
            pltpu.VMEM((groups, owned, owned, tokens), bf16),
            pltpu.VMEM((groups - 1, owned, owned, body), bf16),
            pltpu.VMEM((groups - 1, owned // 2, owned, width), bf16),
            pltpu.VMEM((owned, groups, owned, body), bf16),
            pltpu.VMEM((owned // 2, groups, owned, width), bf16),
            pltpu.VMEM((owned, width, body + width), bf16),
            pltpu.VMEM((owned, width, width), bf16),
            pltpu.VMEM((owned * width, width), f32),
            pltpu.VMEM((owned * width, width), f32),
            pltpu.VMEM((2, rings, 2 * rows, width), f32),
            pltpu.VMEM((2, 2, half, rows, width), f32),
            pltpu.VMEM((2, 2, half - 1, rows, width), f32),
            pltpu.VMEM((2, rows, width), f32),
            *[dma((2, groups - 1))] * 4,
            dma((2, rings)), dma((2, rings)),
            dma((2, 2, half)), dma((2, 2, half)),
            dma((2, 2, half - 1)), dma((2, 2, half - 1)),
            dma((2,)), dma((2,)),
        ],
        compiler_params=pltpu.CompilerParams(
            collective_id=0, has_side_effects=True, vmem_limit_bytes=58 * 1024 * 1024
        ),
        name="monarch_backward",
    )(inputs, left_factor, right_factor, grad_output)

    def restore(out):
        return jnp.transpose(out.reshape(width // replicas, owned, width), (1, 0, 2))

    return grad, restore(left), restore(right)


def solution(mesh):
    return jax.shard_map(
        local,
        mesh=mesh,
        in_specs=(P("dp", "blk"), P("blk", None, None), P("blk", None, None), P("dp", "blk")),
        out_specs=(P("dp", "blk"), P("blk", "dp", None), P("blk", "dp", None)),
        check_vma=False,
    )
```

```python
import functools

import jax
import jax.numpy as jnp
from jax import lax
from jax.experimental import pallas as pl
from jax.experimental.pallas import tpu as pltpu
from jax.sharding import PartitionSpec as P

MESH = pl.DeviceIdType.MESH
OFFSETS = ((2, 1), (2, 0), (1, 1), (3, 1), (1, 0), (3, 0), (0, 1))
LEAD = 2
NN = (((1,), (0,)), ((), ()))
NT = (((1,), (1,)), ((), ()))
TN = (((0,), (0,)), ((), ()))


def dot(a, b, dims):
    return lax.dot_general(a, b, dims, preferred_element_type=jnp.float32)


def swapped(index):
    return (index & ~6) | ((index & 4) >> 1) | ((index & 2) << 1)


def one_hot(rows, pick):
    row = lax.broadcasted_iota(jnp.int32, (rows, rows), 0)
    col = lax.broadcasted_iota(jnp.int32, (rows, rows), 1)
    return jnp.where(col == pick(row), 1.0, 0.0).astype(jnp.bfloat16)


def monarch_kernel(
    scale, rings, x_ref, l_ref, r_ref, g_ref, gin_ref, lo_ref, ro_ref,
    hc, hs, hs_end, hr, hr_end, bc, bs, bs_end, br, br_end, xt, lt, sr, sl, pair, up, down, fold,
    hid_s, hid_r, back_s, back_r,
    pair_s, pair_r, up_s, up_r, down_s, down_r, fold_s, fold_r,
):
    owned, width = l_ref.shape[0], l_ref.shape[1]
    tokens = x_ref.shape[0]
    body = hr.shape[-1]
    rest = tokens - body
    me = lax.axis_index("dp")
    core, high, z = lax.rem(me, 2), lax.rem(me // 2, 2), me // 4
    half = rings // 2
    mate = me + 1 - 2 * core
    across = me + 2 - 4 * high
    above = lax.rem(z + 1, rings) * 4 + high * 2 + core
    below = lax.rem(z + rings - 1, rings) * 4 + high * 2 + core
    blk = lax.axis_index("blk")
    blk_y, blk_x = blk // 4, lax.rem(blk, 4)
    partners = [
        lax.rem(blk_y + dy, 2) * 4 + lax.rem(blk_x + dx, 4) for dx, dy in OFFSETS
    ]

    barrier = pltpu.get_barrier_semaphore()
    for peer in (mate, across, above, below):
        pl.semaphore_signal(barrier, inc=1, device_id={"dp": peer}, device_id_type=MESH)
    for peer in partners:
        pl.semaphore_signal(barrier, inc=1, device_id={"blk": peer}, device_id_type=MESH)

    def send(src, dst, send_sem, recv_sem, axis, peer):
        copy = pltpu.make_async_remote_copy(
            src_ref=src, dst_ref=dst, send_sem=send_sem, recv_sem=recv_sem,
            device_id={axis: peer}, device_id_type=MESH,
        )
        copy.start()
        return copy

    def columns(c):
        return pl.ds(pl.multiple_of(c * width, width), width)

    def split(value):
        return value.astype(jnp.bfloat16).reshape(width // owned, owned, tokens)

    def hidden_block(c, carry):
        lt[c] = l_ref[c].T
        hc[:, c] = split(dot(lt[c], x_ref[:, columns(c)], NT))
        return carry

    def back_block(j, carry):
        bc[:, j] = split(dot(r_ref[j], g_ref[:, columns(j)], NT))
        return carry

    def exchange(blocks, staged, landed, order, send_sem, recv_sem):
        copies = []
        for n, peer in enumerate((*partners, blk)):
            rows = blocks[peer].reshape(owned * owned, tokens)
            moved = dot(order, rows, NN)
            ends = jnp.concatenate([moved[:width, body:], moved[width:, body:]], axis=1)
            pieces = (
                moved[:, :body].astype(jnp.bfloat16).reshape(owned, owned, body),
                ends.astype(jnp.bfloat16).reshape(owned // 2, owned, 2 * rest),
            )
            for part, value in enumerate(pieces):
                if n < len(partners):
                    staged[part][n] = value
                    copies.append(
                        send(
                            staged[part].at[n], landed[part].at[:, blk],
                            send_sem.at[part, n], recv_sem.at[part, n], "blk", peer,
                        )
                    )
                else:
                    landed[part][:, blk] = value
        return copies

    def spread(value, block):
        blank = jnp.zeros_like(value)
        return jnp.concatenate([value, blank] if block < owned // 2 else [blank, value], axis=0)

    lax.fori_loop(0, owned, hidden_block, 0, unroll=2)
    to_right = one_hot(owned * owned, lambda r: (swapped(r & 15) << 4) | (r >> 4))
    pl.semaphore_wait(barrier, 4 + len(partners))
    hidden_copies = exchange(hc, (hs, hs_end), (hr, hr_end), to_right, hid_s, hid_r)
    lax.fori_loop(0, owned, back_block, 0, unroll=2)
    to_left = one_hot(owned * owned, lambda r: ((r & 15) << 4) | (r >> 4))
    back_copies = exchange(bc, (bs, bs_end), (br, br_end), to_left, back_s, back_r)

    turn = one_hot(width, swapped)

    def turn_block(n, carry):
        for first in (0, owned // 2):
            c = n + first
            rows = jnp.concatenate([x_ref[:body, columns(c)], spread(x_ref[body:, columns(c)], first)], axis=0)
            xt[c] = dot(turn, rows, NT).astype(jnp.bfloat16)
        return carry

    lax.fori_loop(0, owned // 2, turn_block, 0)

    order = []
    for step in range(half):
        order.append(lax.rem(z + half - step, rings))
        if step < half - 1:
            order.append(lax.rem(z + rings - (half - 1 - step), rings))
    order.append(z)
    piece = owned * 4

    halves = (1 - high, high)
    slab = piece // 2

    def rows_at(start, count):
        return pl.ds(pl.multiple_of(start, count), count)

    def reduce_lane(lane, ref, out):
        pairs = [
            send(
                ref.at[rows_at(target * (2 * piece) + (1 - core) * piece, piece)], pair.at[lane, k],
                pair_s.at[lane, k], pair_r.at[lane, k], "dp", mate,
            )
            for k, target in enumerate(order)
        ]
        started = list(pairs)

        def own(k, e):
            if e == 0:
                pairs[k].wait_recv()
            start = order[k] * (2 * piece) + core * piece + halves[e] * slab
            return pair[lane, k, rows_at(halves[e] * slab, slab)] + ref[rows_at(start, slab)]

        def advance(step, k, e, before, held, send_sem, recv_sem, peer):
            mine = own(k, e)
            if step == 0:
                source = pair.at[lane, k, rows_at(halves[e] * slab, slab)]
                source[...] = mine
            else:
                before.wait_recv()
                source = held.at[lane, e, step - 1]
                source[...] += mine
            copy = send(
                source, held.at[lane, e, step],
                send_sem.at[lane, e, step], recv_sem.at[lane, e, step], "dp", peer,
            )
            started.append(copy)
            return copy

        rise, sink = [None, None], [None, None]
        for step in range(half):
            for e in range(2):
                rise[e] = advance(step, 2 * step, e, rise[e], up, up_s, up_r, above)
                if step < half - 1:
                    sink[e] = advance(step, 2 * step + 1, e, sink[e], down, down_s, down_r, below)
            yield
        last = pair.at[lane, rings - 1]
        for e in range(2):
            mine = own(rings - 1, e)
            rise[e].wait_recv()
            sink[e].wait_recv()
            total = last.at[rows_at(halves[e] * slab, slab)]
            total[...] = mine + up[lane, e, half - 1] + down[lane, e, half - 2]
            if e == 0:
                folded = send(total, fold.at[lane], fold_s.at[lane], fold_r.at[lane], "dp", across)
                started.append(folded)
        yield
        folded.wait_recv()
        out[...] = (last[rows_at(high * slab, slab)] + fold[lane]) * scale
        for copy in started:
            copy.wait_send()
        yield

    for copy in hidden_copies:
        copy.wait_recv()
    for j in range(owned):
        across_j = slice(j * width, (j + 1) * width)
        ends = hr_end[j % (owned // 2)].reshape(width, 2 * rest)
        sr[pl.ds(j, width, stride=owned), :] = dot(
            hr[j].reshape(width, body), g_ref[:body, across_j], NN
        ) + dot(ends, spread(g_ref[body:, across_j], j), NN)
    right_lane = reduce_lane(0, sr, ro_ref)
    for _ in range(LEAD):
        next(right_lane)

    for copy in back_copies:
        copy.wait_recv()
    for c in range(owned):
        ends = br_end[c % (owned // 2)].reshape(width, 2 * rest)
        sl[pl.ds(c, width, stride=owned), :] = dot(
            xt[c, :, :body], br[c].reshape(width, body), NT
        ) + dot(xt[c, :, body:], ends, NT)

    def grad_in(step):
        for c in range(2 * step, 2 * step + 2):
            across_c = slice(c * width, (c + 1) * width)
            gin_ref[:body, across_c] = dot(br[c].reshape(width, body), lt[c], TN).astype(jnp.bfloat16)
            ends = dot(br_end[c % (owned // 2)].reshape(width, 2 * rest), lt[c], TN)
            first = c // (owned // 2) * rest
            gin_ref[body:, across_c] = ends[first:first + rest].astype(jnp.bfloat16)

    left_lane = reduce_lane(1, sl, lo_ref)
    for step in range(half + 2):
        if step + LEAD < half + 2:
            next(right_lane)
        next(left_lane)
        if step < half:
            grad_in(step)
    for copy in (*hidden_copies, *back_copies):
        copy.wait_send()


def local(inputs, left_factor, right_factor, grad_output):
    replicas = lax.axis_size("dp")
    groups = lax.axis_size("blk")
    tokens = inputs.shape[0]
    owned, width = left_factor.shape[0], left_factor.shape[1]
    scale = float(tokens * replicas) ** (-0.5)
    rings = replicas // 4
    half = rings // 2
    body = tokens - width // 2
    rows = owned * (width // replicas)
    dma = pltpu.SemaphoreType.DMA
    vmem = pl.BlockSpec(memory_space=pltpu.VMEM)
    bf16, f32 = jnp.bfloat16, jnp.float32
    grad, left, right = pl.pallas_call(
        functools.partial(monarch_kernel, scale, rings),
        out_shape=[
            jax.ShapeDtypeStruct(inputs.shape, bf16),
            jax.ShapeDtypeStruct((rows, width), f32),
            jax.ShapeDtypeStruct((rows, width), f32),
        ],
        in_specs=[vmem] * 4,
        out_specs=[vmem] * 3,
        scratch_shapes=[
            pltpu.VMEM((groups, owned, owned, tokens), bf16),
            pltpu.VMEM((groups - 1, owned, owned, body), bf16),
            pltpu.VMEM((groups - 1, owned // 2, owned, width), bf16),
            pltpu.VMEM((owned, groups, owned, body), bf16),
            pltpu.VMEM((owned // 2, groups, owned, width), bf16),
            pltpu.VMEM((groups, owned, owned, tokens), bf16),
            pltpu.VMEM((groups - 1, owned, owned, body), bf16),
            pltpu.VMEM((groups - 1, owned // 2, owned, width), bf16),
            pltpu.VMEM((owned, groups, owned, body), bf16),
            pltpu.VMEM((owned // 2, groups, owned, width), bf16),
            pltpu.VMEM((owned, width, body + width), bf16),
            pltpu.VMEM((owned, width, width), bf16),
            pltpu.VMEM((owned * width, width), f32),
            pltpu.VMEM((owned * width, width), f32),
            pltpu.VMEM((2, rings, 2 * rows, width), f32),
            pltpu.VMEM((2, 2, half, rows, width), f32),
            pltpu.VMEM((2, 2, half - 1, rows, width), f32),
            pltpu.VMEM((2, rows, width), f32),
            *[dma((2, groups - 1))] * 4,
            dma((2, rings)), dma((2, rings)),
            dma((2, 2, half)), dma((2, 2, half)),
            dma((2, 2, half - 1)), dma((2, 2, half - 1)),
            dma((2,)), dma((2,)),
        ],
        compiler_params=pltpu.CompilerParams(
            collective_id=0, has_side_effects=True, vmem_limit_bytes=58 * 1024 * 1024
        ),
        name="monarch_backward",
    )(inputs, left_factor, right_factor, grad_output)

    def restore(out):
        return jnp.transpose(out.reshape(width // replicas, owned, width), (1, 0, 2))

    return grad, restore(left), restore(right)


def solution(mesh):
    return jax.shard_map(
        local,
        mesh=mesh,
        in_specs=(P("dp", "blk"), P("blk", None, None), P("blk", None, None), P("dp", "blk")),
        out_specs=(P("dp", "blk"), P("blk", "dp", None), P("blk", "dp", None)),
        check_vma=False,
    )
```

```python
import functools

import jax
import jax.numpy as jnp
from jax import lax
from jax.experimental import pallas as pl
from jax.experimental.pallas import tpu as pltpu
from jax.sharding import PartitionSpec as P

MESH = pl.DeviceIdType.MESH
OFFSETS = ((2, 1), (2, 0), (1, 1), (3, 1), (1, 0), (3, 0), (0, 1))
LEAD = 2
NN = (((1,), (0,)), ((), ()))
NT = (((1,), (1,)), ((), ()))
TN = (((0,), (0,)), ((), ()))


def dot(a, b, dims):
    return lax.dot_general(a, b, dims, preferred_element_type=jnp.float32)


def swapped(index):
    return (index & ~6) | ((index & 4) >> 1) | ((index & 2) << 1)


def one_hot(rows, pick):
    row = lax.broadcasted_iota(jnp.int32, (rows, rows), 0)
    col = lax.broadcasted_iota(jnp.int32, (rows, rows), 1)
    return jnp.where(col == pick(row), 1.0, 0.0).astype(jnp.bfloat16)


def monarch_kernel(
    scale, rings, x_ref, l_ref, r_ref, g_ref, gin_ref, lo_ref, ro_ref,
    hc, hs, hs_end, hr, hr_end, bc, bs, bs_end, br, br_end, xt, lt, sr, sl, pair, up, down, fold,
    hid_s, hid_r, back_s, back_r,
    pair_s, pair_r, up_s, up_r, down_s, down_r, fold_s, fold_r,
):
    owned, width = l_ref.shape[0], l_ref.shape[1]
    tokens = x_ref.shape[0]
    body = hr.shape[-1]
    rest = tokens - body
    me = lax.axis_index("dp")
    core, high, z = lax.rem(me, 2), lax.rem(me // 2, 2), me // 4
    half = rings // 2
    mate = me + 1 - 2 * core
    across = me + 2 - 4 * high
    above = lax.rem(z + 1, rings) * 4 + high * 2 + core
    below = lax.rem(z + rings - 1, rings) * 4 + high * 2 + core
    blk = lax.axis_index("blk")
    blk_y, blk_x = blk // 4, lax.rem(blk, 4)
    partners = [
        lax.rem(blk_y + dy, 2) * 4 + lax.rem(blk_x + dx, 4) for dx, dy in OFFSETS
    ]

    barrier = pltpu.get_barrier_semaphore()
    for peer in (mate, across, above, below):
        pl.semaphore_signal(barrier, inc=1, device_id={"dp": peer}, device_id_type=MESH)
    for peer in partners:
        pl.semaphore_signal(barrier, inc=1, device_id={"blk": peer}, device_id_type=MESH)

    def send(src, dst, send_sem, recv_sem, axis, peer):
        copy = pltpu.make_async_remote_copy(
            src_ref=src, dst_ref=dst, send_sem=send_sem, recv_sem=recv_sem,
            device_id={axis: peer}, device_id_type=MESH,
        )
        copy.start()
        return copy

    def columns(c):
        return pl.ds(pl.multiple_of(c * width, width), width)

    def split(value):
        return value.astype(jnp.bfloat16).reshape(width // owned, owned, tokens)

    def hidden_block(c, carry):
        lt[c] = l_ref[c].T
        hc[:, c] = split(dot(lt[c], x_ref[:, columns(c)], NT))
        return carry

    def back_block(j, carry):
        bc[:, j] = split(dot(r_ref[j], g_ref[:, columns(j)], NT))
        return carry

    def exchange(blocks, staged, landed, order, send_sem, recv_sem):
        copies = []
        for n, peer in enumerate((*partners, blk)):
            rows = blocks[peer].reshape(owned * owned, tokens)
            moved = dot(order, rows, NN)
            ends = jnp.concatenate([moved[:width, body:], moved[width:, body:]], axis=1)
            pieces = (
                moved[:, :body].astype(jnp.bfloat16).reshape(owned, owned, body),
                ends.astype(jnp.bfloat16).reshape(owned // 2, owned, 2 * rest),
            )
            for part, value in enumerate(pieces):
                if n < len(partners):
                    staged[part][n] = value
                    copies.append(
                        send(
                            staged[part].at[n], landed[part].at[:, blk],
                            send_sem.at[part, n], recv_sem.at[part, n], "blk", peer,
                        )
                    )
                else:
                    landed[part][:, blk] = value
        return copies

    def spread(value, block):
        blank = jnp.zeros_like(value)
        return jnp.concatenate([value, blank] if block < owned // 2 else [blank, value], axis=0)

    lax.fori_loop(0, owned, hidden_block, 0, unroll=4)
    to_right = one_hot(owned * owned, lambda r: (swapped(r & 15) << 4) | (r >> 4))
    pl.semaphore_wait(barrier, 4 + len(partners))
    hidden_copies = exchange(hc, (hs, hs_end), (hr, hr_end), to_right, hid_s, hid_r)
    lax.fori_loop(0, owned, back_block, 0, unroll=4)
    to_left = one_hot(owned * owned, lambda r: ((r & 15) << 4) | (r >> 4))
    back_copies = exchange(bc, (bs, bs_end), (br, br_end), to_left, back_s, back_r)

    turn = one_hot(width, swapped)

    def turn_block(n, carry):
        for first in (0, owned // 2):
            c = n + first
            rows = jnp.concatenate([x_ref[:body, columns(c)], spread(x_ref[body:, columns(c)], first)], axis=0)
            xt[c] = dot(turn, rows, NT).astype(jnp.bfloat16)
        return carry

    lax.fori_loop(0, owned // 2, turn_block, 0)

    order = []
    for step in range(half):
        order.append(lax.rem(z + half - step, rings))
        if step < half - 1:
            order.append(lax.rem(z + rings - (half - 1 - step), rings))
    order.append(z)
    piece = owned * 4

    halves = (1 - high, high)
    slab = piece // 2

    def rows_at(start, count):
        return pl.ds(pl.multiple_of(start, count), count)

    def reduce_lane(lane, ref, out):
        pairs = [
            send(
                ref.at[rows_at(target * (2 * piece) + (1 - core) * piece, piece)], pair.at[lane, k],
                pair_s.at[lane, k], pair_r.at[lane, k], "dp", mate,
            )
            for k, target in enumerate(order)
        ]
        started = list(pairs)

        def own(k, e):
            if e == 0:
                pairs[k].wait_recv()
            start = order[k] * (2 * piece) + core * piece + halves[e] * slab
            return pair[lane, k, rows_at(halves[e] * slab, slab)] + ref[rows_at(start, slab)]

        def advance(step, k, e, before, held, send_sem, recv_sem, peer):
            mine = own(k, e)
            if step == 0:
                source = pair.at[lane, k, rows_at(halves[e] * slab, slab)]
                source[...] = mine
            else:
                before.wait_recv()
                source = held.at[lane, e, step - 1]
                source[...] += mine
            copy = send(
                source, held.at[lane, e, step],
                send_sem.at[lane, e, step], recv_sem.at[lane, e, step], "dp", peer,
            )
            started.append(copy)
            return copy

        rise, sink = [None, None], [None, None]
        for step in range(half):
            for e in range(2):
                rise[e] = advance(step, 2 * step, e, rise[e], up, up_s, up_r, above)
                if step < half - 1:
                    sink[e] = advance(step, 2 * step + 1, e, sink[e], down, down_s, down_r, below)
            yield
        last = pair.at[lane, rings - 1]
        for e in range(2):
            mine = own(rings - 1, e)
            rise[e].wait_recv()
            sink[e].wait_recv()
            total = last.at[rows_at(halves[e] * slab, slab)]
            total[...] = mine + up[lane, e, half - 1] + down[lane, e, half - 2]
            if e == 0:
                folded = send(total, fold.at[lane], fold_s.at[lane], fold_r.at[lane], "dp", across)
                started.append(folded)
        yield
        folded.wait_recv()
        out[...] = (last[rows_at(high * slab, slab)] + fold[lane]) * scale
        for copy in started:
            copy.wait_send()
        yield

    for copy in hidden_copies:
        copy.wait_recv()
    for j in range(owned):
        across_j = slice(j * width, (j + 1) * width)
        ends = hr_end[j % (owned // 2)].reshape(width, 2 * rest)
        sr[pl.ds(j, width, stride=owned), :] = dot(
            hr[j].reshape(width, body), g_ref[:body, across_j], NN
        ) + dot(ends, spread(g_ref[body:, across_j], j), NN)
    right_lane = reduce_lane(0, sr, ro_ref)
    for _ in range(LEAD):
        next(right_lane)

    for copy in back_copies:
        copy.wait_recv()
    for c in range(owned):
        ends = br_end[c % (owned // 2)].reshape(width, 2 * rest)
        sl[pl.ds(c, width, stride=owned), :] = dot(
            xt[c, :, :body], br[c].reshape(width, body), NT
        ) + dot(xt[c, :, body:], ends, NT)

    def grad_in(step):
        for c in range(2 * step, 2 * step + 2):
            across_c = slice(c * width, (c + 1) * width)
            gin_ref[:body, across_c] = dot(br[c].reshape(width, body), lt[c], TN).astype(jnp.bfloat16)
            ends = dot(br_end[c % (owned // 2)].reshape(width, 2 * rest), lt[c], TN)
            first = c // (owned // 2) * rest
            gin_ref[body:, across_c] = ends[first:first + rest].astype(jnp.bfloat16)

    left_lane = reduce_lane(1, sl, lo_ref)
    for step in range(half + 2):
        next(left_lane)
        if step + LEAD < half + 2:
            next(right_lane)
        if step < half:
            grad_in(step)
    for copy in (*hidden_copies, *back_copies):
        copy.wait_send()


def local(inputs, left_factor, right_factor, grad_output):
    replicas = lax.axis_size("dp")
    groups = lax.axis_size("blk")
    tokens = inputs.shape[0]
    owned, width = left_factor.shape[0], left_factor.shape[1]
    scale = float(tokens * replicas) ** (-0.5)
    rings = replicas // 4
    half = rings // 2
    body = tokens - width // 2
    rows = owned * (width // replicas)
    dma = pltpu.SemaphoreType.DMA
    vmem = pl.BlockSpec(memory_space=pltpu.VMEM)
    bf16, f32 = jnp.bfloat16, jnp.float32
    grad, left, right = pl.pallas_call(
        functools.partial(monarch_kernel, scale, rings),
        out_shape=[
            jax.ShapeDtypeStruct(inputs.shape, bf16),
            jax.ShapeDtypeStruct((rows, width), f32),
            jax.ShapeDtypeStruct((rows, width), f32),
        ],
        in_specs=[vmem] * 4,
        out_specs=[vmem] * 3,
        scratch_shapes=[
            pltpu.VMEM((groups, owned, owned, tokens), bf16),
            pltpu.VMEM((groups - 1, owned, owned, body), bf16),
            pltpu.VMEM((groups - 1, owned // 2, owned, width), bf16),
            pltpu.VMEM((owned, groups, owned, body), bf16),
            pltpu.VMEM((owned // 2, groups, owned, width), bf16),
            pltpu.VMEM((groups, owned, owned, tokens), bf16),
            pltpu.VMEM((groups - 1, owned, owned, body), bf16),
            pltpu.VMEM((groups - 1, owned // 2, owned, width), bf16),
            pltpu.VMEM((owned, groups, owned, body), bf16),
            pltpu.VMEM((owned // 2, groups, owned, width), bf16),
            pltpu.VMEM((owned, width, body + width), bf16),
            pltpu.VMEM((owned, width, width), bf16),
            pltpu.VMEM((owned * width, width), f32),
            pltpu.VMEM((owned * width, width), f32),
            pltpu.VMEM((2, rings, 2 * rows, width), f32),
            pltpu.VMEM((2, 2, half, rows, width), f32),
            pltpu.VMEM((2, 2, half - 1, rows, width), f32),
            pltpu.VMEM((2, rows, width), f32),
            *[dma((2, groups - 1))] * 4,
            dma((2, rings)), dma((2, rings)),
            dma((2, 2, half)), dma((2, 2, half)),
            dma((2, 2, half - 1)), dma((2, 2, half - 1)),
            dma((2,)), dma((2,)),
        ],
        compiler_params=pltpu.CompilerParams(
            collective_id=0, has_side_effects=True, vmem_limit_bytes=58 * 1024 * 1024
        ),
        name="monarch_backward",
    )(inputs, left_factor, right_factor, grad_output)

    def restore(out):
        return jnp.transpose(out.reshape(width // replicas, owned, width), (1, 0, 2))

    return grad, restore(left), restore(right)


def solution(mesh):
    return jax.shard_map(
        local,
        mesh=mesh,
        in_specs=(P("dp", "blk"), P("blk", None, None), P("blk", None, None), P("dp", "blk")),
        out_specs=(P("dp", "blk"), P("blk", "dp", None), P("blk", "dp", None)),
        check_vma=False,
    )
```
